512 devices in a mesh: batch: 32 (over y_lo, x, core), width: 16 (over z, y_hi).
Axes of the slice: x: 4, y: 8 (y_hi: 2, y_lo: 4; y = y_hi * 4 + y_lo), z: 8, core: 2. Of those that a mesh axis runs over, the one named last changes fastest.
Arguments:
- samples: bfloat16 [8192, 8192], P('batch', 'width'), parts along dimension 0, may hold values from -6 to 6
- rank_down: bfloat16 [8192, 2, 1024], P('width'), may hold values from -0.09375 to 0.09375
- rank_up: bfloat16 [1024, 2, 8192], P(None, None, 'width'), may hold values from -0.1875 to 0.1875
- gate_proj: bfloat16 [8192, 2], P('width'), may hold values from -0.0625 to 0.0625
- expert_bias: float32 [2, 8192], P(None, 'width'), may hold values from -3 to 3
Outputs:
- crossed: bfloat16 [8192, 8192], P('batch', 'width'), parts along dimension 0
The draws below stay inside these ranges and needn't reach their ends.
There are 32 independent parts, one for each index of `batch`. The reference program is written for one: setup_inputs(seed, part) draws one part's arguments, and reference() takes and returns one part's arrays. A program takes and returns all parts, laid end to end along the dimension named above; an argument that names none is the same for every part. Nothing has to cross between parts.
All inputs are finite; a program needn't handle non-finite values.
Results may differ from the reference program's by a relative error of at most 0.0027.
Values may be sent and summed in bfloat16 or wider, within the bound.
A program may use at most 64 MiB of HBM per device.

```python
import jax
import jax.numpy as jnp

D = 8192
RANK = 1024
EXPERTS = 2
ROWS = 256


def with_spikes(drawn, stream_key, source, target, parts, factor):
    owner, partner = [(jnp.arange(drawn.shape[position]) // (drawn.shape[position] // parts)).reshape([-1 if axis == position else 1 for axis in range(drawn.ndim)]) for position in (source, target)]
    chosen = jax.random.permutation(stream_key, parts)[partner]
    strong = (owner == chosen) | (owner == (partner + parts // 2) % parts)
    return jnp.where(strong, factor * drawn, drawn)


def steps_of(own_key, shape, split, smallest, high):
    def one(axis_at, blocks):
        heights = jax.random.uniform(jax.random.fold_in(jax.random.fold_in(own_key, 6), axis_at), (blocks,), jnp.float32, smallest / len(split), high / len(split))
        return jnp.repeat(jnp.exp(heights), shape[axis_at] // blocks).reshape((-1,) + (1,) * (len(shape) - axis_at - 1))

    loudness = one(*split[0])
    for cut in split[1:]:
        loudness = loudness * one(*cut)
    return loudness


def normal_values(rng, extent, width, most, pieces=(), kind=jnp.bfloat16):
    result = jax.random.normal(rng, extent, jnp.float32) * width
    if len(pieces) > 0:
        result = steps_of(rng, extent, pieces, -0.22, 0.18) * result
    return jnp.clip(result, min=-most, max=most).astype(kind)


def bell_draw_with(own_key, extent, deviation, bound, pieces, heavy, dtype=jnp.bfloat16):
    entries = deviation * jax.random.normal(own_key, extent, jnp.float32)
    if pieces:
        entries = entries * steps_of(own_key, extent, pieces, -0.22, 0.18)
    return jnp.clip(with_spikes(entries, jax.random.fold_in(own_key, 3), *heavy), -bound, bound).astype(dtype)


def setup_inputs(seed: int = 0, part: int = 0) -> dict:
    keys = jax.random.split(jax.random.key(seed), 6)
    part_splits = jax.random.split(jax.random.fold_in(keys[5], part), 6)
    return {
        "samples": normal_values(part_splits[0], (ROWS, D), 1.0, 6.0, ((1, 16),)),
        "rank_down": bell_draw_with(keys[1], (D, EXPERTS, RANK), D ** -0.5, 0.09375, ((0, 16),), (0, 2, 16, 2.0)),
        "rank_up": normal_values(keys[2], (RANK, EXPERTS, D), RANK ** -0.5, 0.1875, ((2, 16),)),
        "gate_proj": normal_values(keys[3], (D, EXPERTS), D ** -0.5, 0.0625, ((0, 16),)),
        "expert_bias": normal_values(keys[4], (EXPERTS, D), 0.5, 3.0, ((1, 16),), jnp.float32),
    }


def reference(samples, rank_down, rank_up, gate_proj, expert_bias):
    inputs = samples.astype(jnp.float32)
    reduced = jnp.einsum("bf,fek->bek", inputs, rank_down.astype(jnp.float32))
    hidden = jnp.tanh(reduced).astype(jnp.bfloat16)
    logits = jnp.dot(samples, gate_proj, preferred_element_type=jnp.float32)
    gating = jax.nn.sigmoid(logits)
    expanded = jnp.einsum("bek,kef->ebf", hidden.astype(jnp.float32), rank_up.astype(jnp.float32))
    blended = jnp.sum(jnp.transpose(gating)[:, :, None] * (expanded + expert_bias[:, None, :]), axis=0)
    return (inputs * blended + inputs).astype(jnp.bfloat16)
```

```python
import functools

import jax
import jax.numpy as jnp
from jax import lax
from jax.experimental import pallas as pl
from jax.experimental.pallas import tpu as pltpu
from jax.sharding import PartitionSpec as P

MESH = pl.DeviceIdType.MESH
BF = jnp.bfloat16
F32 = jnp.float32
RING = 8
PIECES = ((0, 0), (0, 1), (1, 0), (1, 1))
ORDER = (4, 3, -3, 2, -2, 1, -1, 0)
TREES = ((0, 0, 1, 2, 3), (0, 0, 1, 2, 3))


def reach(direction, expert):
    return 4 if (direction == 0) == (expert == 0) else 3


def block(d, distance):
    return ORDER.index(distance if d == 0 or distance in (0, 4) else -distance)


def rows_of(e, h):
    return slice(e * 256 + h * 128, e * 256 + h * 128 + 128)


def kernel(
    x_hbm, w_hbm, u_hbm, gate_hbm, bias_hbm, out_ref,
    x, w, u, gate, bias, xe, part, send, recv, ysend, yrecv, hid, got, logit, lrecv, lsum, lsum_r, acc,
    x_sem, w_sem, u_sem, g_sem, b_sem,
    rs_s, rs_r, y_s, y_r, ag_s, ag_r, l_s, l_r,
):
    me = lax.axis_index("width")
    z = me // 2
    y = lax.rem(me, 2)
    core = lax.rem(lax.axis_index("batch"), 2)

    def at(offset):
        return lax.rem(z + offset + RING, RING)

    def dev(offset):
        return {"width": at(offset) * 2 + y}

    mate = {"width": z * 2 + (1 - y)}

    barrier = pltpu.get_barrier_semaphore()
    x_copy = pltpu.make_async_copy(x_hbm, x, x_sem)
    x_copy.start()
    w_rows = w_hbm.reshape(1024, 1024)
    w_copies = []
    for t, offset in enumerate(ORDER):
        lanes = pl.ds(pl.multiple_of(at(offset) * 128, 128), 128)
        w_copies.append(
            pltpu.make_async_copy(w_rows.at[:, lanes], w.at[:, pl.ds(t * 128, 128)], w_sem.at[t])
        )
        w_copies[-1].start()
    pl.semaphore_signal(barrier, inc=1, device_id=mate, device_id_type=MESH)
    for offset in (1, -1):
        pl.semaphore_signal(barrier, inc=1, device_id=dev(offset), device_id_type=MESH)
    g_copy = pltpu.make_async_copy(gate_hbm, gate, g_sem)
    g_copy.start()
    b_copy = pltpu.make_async_copy(bias_hbm, bias, b_sem)
    b_copy.start()
    u_copy = pltpu.make_async_copy(u_hbm.reshape(2048, 512), u, u_sem)
    u_copy.start()

    row = lax.broadcasted_iota(jnp.int32, (128, 256), 0)
    lane = lax.broadcasted_iota(jnp.int32, (128, 256), 1)
    pick = [jnp.where(lane == 2 * row + e, 1.0, 0.0).astype(BF) for e in range(2)]

    x_copy.wait()
    for e in range(2):
        for c in range(4):
            xe[e * 256 : (e + 1) * 256, c * 256 : (c + 1) * 256] = jnp.dot(
                x[:, c * 128 : (c + 1) * 128], pick[e], preferred_element_type=F32
            ).astype(BF)

    def product(p):
        w_copies[2 * p].wait()
        w_copies[2 * p + 1].wait()
        part[p] = jnp.dot(xe[...], w[:, p * 256 : (p + 1) * 256], preferred_element_type=F32)

    def part_of(t, e, h):
        return part[t // 2, rows_of(e, h), (t % 2) * 128 : (t % 2) * 128 + 128]

    def exchange(tree):
        started = []

        def height(k, n):
            below = [height(c, n) + 1 for c in range(1, n + 1) if tree[c] == k]
            return max(below, default=0)

        def depth(k):
            return 0 if k == 0 else depth(tree[k]) + 1

        def children(k, n):
            return [c for c in range(1, n + 1) if tree[c] == k]

        def rs_copy(d, k, i):
            hop = k - tree[k]
            return pltpu.make_async_remote_copy(
                src_ref=send.at[d, k - 1, i], dst_ref=recv.at[d, k - 1, i],
                send_sem=rs_s.at[d, k - 1, i], recv_sem=rs_r.at[d, k - 1, i],
                device_id=dev(hop if d == 0 else -hop), device_id_type=MESH,
            )

        def rs_sum(d, k, i, value):
            for c in children(k, reach(d, PIECES[i][0])):
                rs_copy(d, c, i).wait_recv()
                value = value + recv[d, c - 1, i].astype(F32)
            return value

        def rs_step(d, k, i):
            e, h = PIECES[i]
            send[d, k - 1, i] = rs_sum(d, k, i, part_of(block(d, k), e, h)).astype(BF)
            copy = rs_copy(d, k, i)
            copy.start()
            started.append(copy)

        def rs_level(level):
            for k in (4, 3, 2, 1):
                for i, (e, h) in enumerate(PIECES):
                    for d in range(2):
                        n = reach(d, e)
                        if k <= n and height(k, n) == level:
                            yield d, k, i

        def l_copy(d, r):
            return pltpu.make_async_remote_copy(
                src_ref=logit if r == 0 else lrecv.at[d, r - 1], dst_ref=lrecv.at[d, r],
                send_sem=l_s.at[d, r], recv_sem=l_r.at[d, r],
                device_id=dev(1 if d == 0 else -1), device_id_type=MESH,
            )

        steps = [list(rs_level(level)) for level in range(4)]
        have = 0
        for level in range(4):
            for d, k, i in steps[level]:
                while have <= block(d, k) // 2:
                    product(have)
                    have += 1
                    if have == 1:
                        pl.semaphore_wait(barrier, 3)
                rs_step(d, k, i)
            if level == 0:
                g_copy.wait()
                logit[...] = lax.dot_general(
                    gate[...], x[...], (((1,), (1,)), ((), ())), preferred_element_type=F32
                )
            for d in range(2 if level < 3 else 1):
                if level > 0:
                    l_copy(d, level - 1).wait_recv()
                copy = l_copy(d, level)
                copy.start()
                started.append(copy)
        while have < 4:
            product(have)
            have += 1

        def y_copy(i):
            return pltpu.make_async_remote_copy(
                src_ref=ysend.at[i], dst_ref=yrecv.at[i], send_sem=y_s.at[i], recv_sem=y_r.at[i],
                device_id=mate, device_id_type=MESH,
            )

        for i, (e, h) in enumerate(PIECES):
            total = part_of(7, e, h)
            for d in (1, 0) if e == 0 else (0, 1):
                total = rs_sum(d, 0, i, total)
            part[3, rows_of(e, h), 128:256] = total
            ysend[i] = total.astype(BF)
            copy = y_copy(i)
            copy.start()
            started.append(copy)

        total = logit[...]
        l_copy(0, 3).wait_recv()
        l_copy(1, 2).wait_recv()
        for d in range(2):
            for r in range(4 - d):
                total = total + lrecv[d, r]
        lsum[...] = total
        l_last = pltpu.make_async_remote_copy(
            src_ref=lsum, dst_ref=lsum_r, send_sem=l_s.at[1, 3], recv_sem=l_r.at[1, 3],
            device_id=mate, device_id_type=MESH,
        )
        l_last.start()
        b_copy.wait()
        for e in range(2):
            acc[e] = jnp.broadcast_to(bias[e : e + 1, :], (256, 512))
        u_copy.wait()

        def ag_copy(d, k, i):
            hop = k - tree[k]
            return pltpu.make_async_remote_copy(
                src_ref=hid.at[i] if tree[k] == 0 else got.at[d, tree[k] - 1, i],
                dst_ref=got.at[d, k - 1, i],
                send_sem=ag_s.at[d, k - 1, i], recv_sem=ag_r.at[d, k - 1, i],
                device_id=dev(hop if d == 0 else -hop), device_id_type=MESH,
            )

        def forward(d, k, i):
            for c in sorted(children(k, reach(d, PIECES[i][0])), reverse=True):
                copy = ag_copy(d, c, i)
                copy.start()
                started.append(copy)

        def expand(values, e, source):
            wide = jnp.dot(values, pick[e], preferred_element_type=F32).astype(BF)
            rows = pl.ds(pl.multiple_of(source * 256, 256), 256)
            acc[e] += jnp.dot(wide, u[rows, :], preferred_element_type=F32)

        for i, (e, h) in enumerate(PIECES):
            y_copy(i).wait_recv()
            hid[i] = jnp.tanh(part[3, rows_of(e, h), 128:256] + yrecv[i].astype(F32)).astype(BF)
            for d in range(2):
                forward(d, 0, i)

        for e in range(2):
            expand(jnp.concatenate([hid[2 * e], hid[2 * e + 1]], axis=0), e, at(0))

        l_last.wait_recv()
        gating = 1.0 / (1.0 + jnp.exp(-(lsum[...] + lsum_r[...])))
        eye = lax.broadcasted_iota(jnp.int32, (128, 128), 0) == lax.broadcasted_iota(
            jnp.int32, (128, 128), 1
        )

        def arrive(level):
            for k in (1, 2, 3, 4):
                if depth(k) != level:
                    continue
                for e in range(2):
                    for d in (0, 1) if e == 0 else (1, 0):
                        if reach(d, e) >= k:
                            for h in range(2):
                                ag_copy(d, k, 2 * e + h).wait_recv()
                                forward(d, k, 2 * e + h)

        def absorb(level):
            for k in (1, 2, 3, 4):
                for e in range(2):
                    for d in (0, 1) if e == 0 else (1, 0):
                        if reach(d, e) >= k and depth(k) == level:
                            expand(
                                jnp.concatenate([got[d, k - 1, 2 * e], got[d, k - 1, 2 * e + 1]], axis=0),
                                e,
                                at(-k if d == 0 else k),
                            )

        for level in range(1, 5):
            arrive(level)
            absorb(level)

        for h in range(2):
            rows = slice(h * 128, h * 128 + 128)
            blended = None
            for e in range(2):
                line = jnp.broadcast_to(gating[e : e + 1, h * 128 : h * 128 + 128], (128, 128))
                column = jnp.sum(jnp.where(eye, line, 0.0), axis=1, keepdims=True)
                term = column * acc[e, rows, :]
                blended = term if blended is None else blended + term
            inputs = x[rows, :].astype(F32)
            out_ref[rows, :] = (inputs * blended + inputs).astype(BF)

        for copy in started:
            copy.wait_send()
        l_last.wait_send()

    if TREES[0] == TREES[1]:
        exchange(TREES[0])
    else:
        for c in range(2):
            pl.when(core == c)(functools.partial(exchange, TREES[c]))


def shards(samples, rank_down, rank_up, gate_proj, expert_bias):
    dma = pltpu.SemaphoreType.DMA
    return pl.pallas_call(
        kernel,
        out_shape=pltpu.VMEM(samples.shape, samples.dtype),
        in_specs=[pl.BlockSpec(memory_space=pl.ANY)] * 5,
        out_specs=pl.BlockSpec(memory_space=pltpu.VMEM),
        scratch_shapes=[
            pltpu.VMEM((256, 512), BF),
            pltpu.VMEM((1024, 1024), BF),
            pltpu.VMEM((2048, 512), BF),
            pltpu.VMEM((2, 512), BF),
            pltpu.VMEM((2, 512), F32),
            pltpu.VMEM((512, 1024), BF),
            pltpu.VMEM((4, 512, 256), F32),
            pltpu.VMEM((2, 4, 4, 128, 128), BF),
            pltpu.VMEM((2, 4, 4, 128, 128), BF),
            pltpu.VMEM((4, 128, 128), BF),
            pltpu.VMEM((4, 128, 128), BF),
            pltpu.VMEM((4, 128, 128), BF),
            pltpu.VMEM((2, 4, 4, 128, 128), BF),
            pltpu.VMEM((2, 256), F32),
            pltpu.VMEM((2, 4, 2, 256), F32),
            pltpu.VMEM((2, 256), F32),
            pltpu.VMEM((2, 256), F32),
            pltpu.VMEM((2, 256, 512), F32),
            dma(()),
            dma((8,)),
            dma(()),
            dma(()),
            dma(()),
            dma((2, 4, 4)),
            dma((2, 4, 4)),
            dma((4,)),
            dma((4,)),
            dma((2, 4, 4)),
            dma((2, 4, 4)),
            dma((2, 4)),
            dma((2, 4)),
        ],
        compiler_params=pltpu.CompilerParams(collective_id=0, has_side_effects=True),
        name="cross_experts",
    )(samples, rank_down, rank_up, gate_proj.T, expert_bias)


def solution(mesh):
    placed = (
        P("batch", "width"),
        P("width", None, None),
        P(None, None, "width"),
        P("width", None),
        P(None, "width"),
    )
    return jax.shard_map(
        shards, mesh=mesh, in_specs=placed, out_specs=P("batch", "width"), check_vma=False
    )
```

```python
import functools

import jax
import jax.numpy as jnp
from jax import lax
from jax.experimental import pallas as pl
from jax.experimental.pallas import tpu as pltpu
from jax.sharding import PartitionSpec as P

MESH = pl.DeviceIdType.MESH
BF = jnp.bfloat16
F32 = jnp.float32
RING = 8
CUTS = 2
TALL = 256 // CUTS
PIECES = tuple((e, h) for e in range(2) for h in range(CUTS))
ORDER = (4, 3, -3, 2, -2, 1, -1, 0)
TREES = ((0, 0, 1, 2, 3), (0, 0, 1, 2, 3))


def reach(direction, expert):
    return 4 if (direction == 0) == (expert == 0) else 3


def block(d, distance):
    return ORDER.index(distance if d == 0 or distance in (0, 4) else -distance)


def rows_of(e, h):
    return slice(e * 256 + h * TALL, e * 256 + h * TALL + TALL)


def piece(ref, i):
    e, h = PIECES[i]
    return ref.at[e, pl.ds(h * TALL, TALL)]


def kernel(
    x_hbm, w_hbm, u_hbm, gate_hbm, bias_hbm, out_ref,
    x, w, u, gate, bias, xe, part, send, recv, ysend, yrecv, hid, got, logit, lrecv, lsum, lsum_r, acc,
    x_sem, w_sem, u_sem, g_sem, b_sem,
    rs_s, rs_r, y_s, y_r, ag_s, ag_r, l_s, l_r,
):
    me = lax.axis_index("width")
    z = me // 2
    y = lax.rem(me, 2)
    core = lax.rem(lax.axis_index("batch"), 2)

    def at(offset):
        return lax.rem(z + offset + RING, RING)

    def dev(offset):
        return {"width": at(offset) * 2 + y}

    mate = {"width": z * 2 + (1 - y)}

    barrier = pltpu.get_barrier_semaphore()
    x_copy = pltpu.make_async_copy(x_hbm, x, x_sem)
    x_copy.start()
    w_rows = w_hbm.reshape(1024, 1024)
    w_copies = []
    for t, offset in enumerate(ORDER):
        lanes = pl.ds(pl.multiple_of(at(offset) * 128, 128), 128)
        w_copies.append(
            pltpu.make_async_copy(w_rows.at[:, lanes], w.at[:, pl.ds(t * 128, 128)], w_sem.at[t])
        )
        w_copies[-1].start()
    pl.semaphore_signal(barrier, inc=1, device_id=mate, device_id_type=MESH)
    for offset in (1, -1):
        pl.semaphore_signal(barrier, inc=1, device_id=dev(offset), device_id_type=MESH)
    g_copy = pltpu.make_async_copy(gate_hbm, gate, g_sem)
    g_copy.start()
    b_copy = pltpu.make_async_copy(bias_hbm, bias, b_sem)
    b_copy.start()
    u_copy = pltpu.make_async_copy(u_hbm.reshape(2048, 512), u, u_sem)
    u_copy.start()

    row = lax.broadcasted_iota(jnp.int32, (128, 256), 0)
    lane = lax.broadcasted_iota(jnp.int32, (128, 256), 1)
    pick = [jnp.where(lane == 2 * row + e, 1.0, 0.0).astype(BF) for e in range(2)]

    x_copy.wait()
    for e in range(2):
        for c in range(4):
            xe[e * 256 : (e + 1) * 256, c * 256 : (c + 1) * 256] = jnp.dot(
                x[:, c * 128 : (c + 1) * 128], pick[e], preferred_element_type=F32
            ).astype(BF)

    def product(p, e):
        if e == 0:
            w_copies[2 * p].wait()
            w_copies[2 * p + 1].wait()
        rows = slice(e * 256, e * 256 + 256)
        part[p, rows, :] = jnp.dot(
            xe[rows, :], w[:, p * 256 : (p + 1) * 256], preferred_element_type=F32
        )

    def part_of(t, e, h):
        return part[t // 2, rows_of(e, h), (t % 2) * 128 : (t % 2) * 128 + 128]

    def exchange(tree):
        started = []

        def height(k, n):
            below = [height(c, n) + 1 for c in range(1, n + 1) if tree[c] == k]
            return max(below, default=0)

        def depth(k):
            return 0 if k == 0 else depth(tree[k]) + 1

        def children(k, n):
            return [c for c in range(1, n + 1) if tree[c] == k]

        def rs_copy(d, k, i):
            hop = k - tree[k]
            return pltpu.make_async_remote_copy(
                src_ref=piece(send.at[d, k - 1], i), dst_ref=piece(recv.at[d, k - 1], i),
                send_sem=rs_s.at[d, k - 1, i], recv_sem=rs_r.at[d, k - 1, i],
                device_id=dev(hop if d == 0 else -hop), device_id_type=MESH,
            )

        def rs_sum(d, k, i, value):
            for c in children(k, reach(d, PIECES[i][0])):
                rs_copy(d, c, i).wait_recv()
                value = value + piece(recv.at[d, c - 1], i)[...].astype(F32)
            return value

        def rs_step(d, k, i):
            e, h = PIECES[i]
            piece(send.at[d, k - 1], i)[...] = rs_sum(d, k, i, part_of(block(d, k), e, h)).astype(BF)
            copy = rs_copy(d, k, i)
            copy.start()
            started.append(copy)

        def rs_round(level, expert):
            for k in (4, 3, 2, 1):
                for i, (e, h) in enumerate(PIECES):
                    for d in range(2):
                        n = reach(d, e)
                        if e == expert and k <= n and height(k, n) == level:
                            rs_step(d, k, i)

        def l_copy(d, r):
            return pltpu.make_async_remote_copy(
                src_ref=logit if r == 0 else lrecv.at[d, r - 1], dst_ref=lrecv.at[d, r],
                send_sem=l_s.at[d, r], recv_sem=l_r.at[d, r],
                device_id=dev(1 if d == 0 else -1), device_id_type=MESH,
            )

        def logit_round(r):
            for d in range(2 if r < 3 else 1):
                if r > 0:
                    l_copy(d, r - 1).wait_recv()
                copy = l_copy(d, r)
                copy.start()
                started.append(copy)

        product(0, 0)
        product(1, 0)
        pl.semaphore_wait(barrier, 3)
        rs_round(0, 0)
        product(0, 1)
        product(1, 1)
        product(2, 0)
        product(2, 1)
        product(3, 0)
        product(3, 1)
        g_copy.wait()
        logit[...] = lax.dot_general(
            gate[...], x[...], (((1,), (1,)), ((), ())), preferred_element_type=F32
        )
        logit_round(0)

        rs_round(0, 1)
        for level in range(1, 4):
            rs_round(level, 0)
            rs_round(level, 1)
            logit_round(level)

        def y_copy(i):
            return pltpu.make_async_remote_copy(
                src_ref=piece(ysend, i), dst_ref=piece(yrecv, i), send_sem=y_s.at[i], recv_sem=y_r.at[i],
                device_id=mate, device_id_type=MESH,
            )

        for i, (e, h) in enumerate(PIECES):
            total = part_of(7, e, h)
            for d in (1, 0) if e == 0 else (0, 1):
                total = rs_sum(d, 0, i, total)
            part[3, rows_of(e, h), 128:256] = total
            piece(ysend, i)[...] = total.astype(BF)
            copy = y_copy(i)
            copy.start()
            started.append(copy)

        total = logit[...]
        l_copy(0, 3).wait_recv()
        l_copy(1, 2).wait_recv()
        for d in range(2):
            for r in range(4 - d):
                total = total + lrecv[d, r]
        lsum[...] = total
        l_last = pltpu.make_async_remote_copy(
            src_ref=lsum, dst_ref=lsum_r, send_sem=l_s.at[1, 3], recv_sem=l_r.at[1, 3],
            device_id=mate, device_id_type=MESH,
        )
        l_last.start()
        b_copy.wait()
        for e in range(2):
            acc[e] = jnp.broadcast_to(bias[e : e + 1, :], (256, 512))
        u_copy.wait()

        def ag_copy(d, k, i):
            hop = k - tree[k]
            return pltpu.make_async_remote_copy(
                src_ref=piece(hid if tree[k] == 0 else got.at[d, tree[k] - 1], i),
                dst_ref=piece(got.at[d, k - 1], i),
                send_sem=ag_s.at[d, k - 1, i], recv_sem=ag_r.at[d, k - 1, i],
                device_id=dev(hop if d == 0 else -hop), device_id_type=MESH,
            )

        def forward(d, k, i):
            for c in sorted(children(k, reach(d, PIECES[i][0])), reverse=True):
                copy = ag_copy(d, c, i)
                copy.start()
                started.append(copy)

        def expand(values, e, source):
            wide = jnp.dot(values, pick[e], preferred_element_type=F32).astype(BF)
            rows = pl.ds(pl.multiple_of(source * 256, 256), 256)
            acc[e] += jnp.dot(wide, u[rows, :], preferred_element_type=F32)

        for i, (e, h) in enumerate(PIECES):
            y_copy(i).wait_recv()
            piece(hid, i)[...] = jnp.tanh(
                part[3, rows_of(e, h), 128:256] + piece(yrecv, i)[...].astype(F32)
            ).astype(BF)
            for d in range(2):
                forward(d, 0, i)
            if h == CUTS - 1:
                expand(hid[e], e, at(0))

        l_last.wait_recv()
        gating = 1.0 / (1.0 + jnp.exp(-(lsum[...] + lsum_r[...])))
        eye = lax.broadcasted_iota(jnp.int32, (128, 128), 0) == lax.broadcasted_iota(
            jnp.int32, (128, 128), 1
        )

        def sources(level, e):
            for k in (1, 2, 3, 4):
                for d in (0, 1) if e == 0 else (1, 0):
                    if reach(d, e) >= k and depth(k) == level:
                        yield d, k

        def arrive(level, e):
            for d, k in sources(level, e):
                for h in range(CUTS):
                    ag_copy(d, k, CUTS * e + h).wait_recv()
                    forward(d, k, CUTS * e + h)

        def absorb(level, e):
            for d, k in sources(level, e):
                expand(got[d, k - 1, e], e, at(-k if d == 0 else k))

        for level in range(1, 5):
            for e in range(2):
                arrive(level, e)
                absorb(level, e)

        for h in range(2):
            rows = slice(h * 128, h * 128 + 128)
            blended = None
            for e in range(2):
                line = jnp.broadcast_to(gating[e : e + 1, h * 128 : h * 128 + 128], (128, 128))
                column = jnp.sum(jnp.where(eye, line, 0.0), axis=1, keepdims=True)
                term = column * acc[e, rows, :]
                blended = term if blended is None else blended + term
            inputs = x[rows, :].astype(F32)
            out_ref[rows, :] = (inputs * blended + inputs).astype(BF)

        for copy in started:
            copy.wait_send()
        l_last.wait_send()

    if TREES[0] == TREES[1]:
        exchange(TREES[0])
    else:
        for c in range(2):
            pl.when(core == c)(functools.partial(exchange, TREES[c]))


def shards(samples, rank_down, rank_up, gate_proj, expert_bias):
    dma = pltpu.SemaphoreType.DMA
    return pl.pallas_call(
        kernel,
        out_shape=pltpu.VMEM(samples.shape, samples.dtype),
        in_specs=[pl.BlockSpec(memory_space=pl.ANY)] * 5,
        out_specs=pl.BlockSpec(memory_space=pltpu.VMEM),
        scratch_shapes=[
            pltpu.VMEM((256, 512), BF),
            pltpu.VMEM((1024, 1024), BF),
            pltpu.VMEM((2048, 512), BF),
            pltpu.VMEM((2, 512), BF),
            pltpu.VMEM((2, 512), F32),
            pltpu.VMEM((512, 1024), BF),
            pltpu.VMEM((4, 512, 256), F32),
            pltpu.VMEM((2, 4, 2, 256, 128), BF),
            pltpu.VMEM((2, 4, 2, 256, 128), BF),
            pltpu.VMEM((2, 256, 128), BF),
            pltpu.VMEM((2, 256, 128), BF),
            pltpu.VMEM((2, 256, 128), BF),
            pltpu.VMEM((2, 4, 2, 256, 128), BF),
            pltpu.VMEM((2, 256), F32),
            pltpu.VMEM((2, 4, 2, 256), F32),
            pltpu.VMEM((2, 256), F32),
            pltpu.VMEM((2, 256), F32),
            pltpu.VMEM((2, 256, 512), F32),
            dma(()),
            dma((8,)),
            dma(()),
            dma(()),
            dma(()),
            dma((2, 4, 2 * CUTS)),
            dma((2, 4, 2 * CUTS)),
            dma((2 * CUTS,)),
            dma((2 * CUTS,)),
            dma((2, 4, 2 * CUTS)),
            dma((2, 4, 2 * CUTS)),
            dma((2, 4)),
            dma((2, 4)),
        ],
        compiler_params=pltpu.CompilerParams(collective_id=0, has_side_effects=True),
        name="cross_experts",
    )(samples, rank_down, rank_up, gate_proj.T, expert_bias)


def solution(mesh):
    placed = (
        P("batch", "width"),
        P("width", None, None),
        P(None, None, "width"),
        P("width", None),
        P(None, "width"),
    )
    return jax.shard_map(
        shards, mesh=mesh, in_specs=placed, out_specs=P("batch", "width"), check_vma=False
    )
```

```python
import functools

import jax
import jax.numpy as jnp
from jax import lax
from jax.experimental import pallas as pl
from jax.experimental.pallas import tpu as pltpu
from jax.sharding import PartitionSpec as P

MESH = pl.DeviceIdType.MESH
BF = jnp.bfloat16
F32 = jnp.float32
RING = 8
CUTS = 2
TALL = 256 // CUTS
PIECES = tuple((e, h) for e in range(2) for h in range(CUTS))
ORDER = (4, 3, -3, 2, -2, 1, -1, 0)
TREES = ((0, 0, 1, 2, 3), (0, 0, 1, 2, 3))


def reach(direction, expert):
    return 4 if (direction == 0) == (expert == 0) else 3


def block(d, distance):
    return ORDER.index(distance if d == 0 or distance in (0, 4) else -distance)


def rows_of(e, h):
    return slice(e * 256 + h * TALL, e * 256 + h * TALL + TALL)


def piece(ref, i):
    e, h = PIECES[i]
    return ref.at[e, pl.ds(h * TALL, TALL)]


def kernel(
    x_hbm, w_hbm, u_hbm, gate_hbm, bias_hbm, out_ref,
    x, w, u, gate, bias, xe, part, send, recv, ysend, yrecv, hid, got, logit, lrecv, lsum, lsum_r, acc, weight,
    x_sem, w_sem, u_sem, g_sem, b_sem,
    rs_s, rs_r, y_s, y_r, ag_s, ag_r, l_s, l_r,
):
    me = lax.axis_index("width")
    z = me // 2
    y = lax.rem(me, 2)
    core = lax.rem(lax.axis_index("batch"), 2)

    def at(offset):
        return lax.rem(z + offset + RING, RING)

    def dev(offset):
        return {"width": at(offset) * 2 + y}

    mate = {"width": z * 2 + (1 - y)}

    barrier = pltpu.get_barrier_semaphore()
    x_copy = pltpu.make_async_copy(x_hbm, x, x_sem)
    x_copy.start()
    w_rows = w_hbm.reshape(1024, 1024)
    w_copies = []
    for t, offset in enumerate(ORDER):
        lanes = pl.ds(pl.multiple_of(at(offset) * 128, 128), 128)
        w_copies.append(
            pltpu.make_async_copy(w_rows.at[:, lanes], w.at[:, pl.ds(t * 128, 128)], w_sem.at[t])
        )
        w_copies[-1].start()
    pl.semaphore_signal(barrier, inc=1, device_id=mate, device_id_type=MESH)
    for offset in (1, -1):
        pl.semaphore_signal(barrier, inc=1, device_id=dev(offset), device_id_type=MESH)
    g_copy = pltpu.make_async_copy(gate_hbm, gate, g_sem)
    g_copy.start()
    b_copy = pltpu.make_async_copy(bias_hbm, bias, b_sem)
    b_copy.start()
    u_copy = pltpu.make_async_copy(u_hbm.reshape(2048, 512), u, u_sem)
    u_copy.start()

    row = lax.broadcasted_iota(jnp.int32, (128, 256), 0)
    lane = lax.broadcasted_iota(jnp.int32, (128, 256), 1)
    pick = [jnp.where(lane == 2 * row + e, 1.0, 0.0).astype(BF) for e in range(2)]

    x_copy.wait()
    for e in range(2):
        for c in range(4):
            xe[e * 256 : (e + 1) * 256, c * 256 : (c + 1) * 256] = jnp.dot(
                x[:, c * 128 : (c + 1) * 128], pick[e], preferred_element_type=F32
            ).astype(BF)

    def product(p, e):
        if e == 0:
            w_copies[2 * p].wait()
            w_copies[2 * p + 1].wait()
        rows = slice(e * 256, e * 256 + 256)
        part[p, rows, :] = jnp.dot(
            xe[rows, :], w[:, p * 256 : (p + 1) * 256], preferred_element_type=F32
        )

    def part_of(t, e, h):
        return part[t // 2, rows_of(e, h), (t % 2) * 128 : (t % 2) * 128 + 128]

    def exchange(tree):
        started = []

        def height(k, n):
            below = [height(c, n) + 1 for c in range(1, n + 1) if tree[c] == k]
            return max(below, default=0)

        def depth(k):
            return 0 if k == 0 else depth(tree[k]) + 1

        def children(k, n):
            return [c for c in range(1, n + 1) if tree[c] == k]

        def rs_copy(d, k, i):
            hop = k - tree[k]
            return pltpu.make_async_remote_copy(
                src_ref=piece(send.at[d, k - 1], i), dst_ref=piece(recv.at[d, k - 1], i),
                send_sem=rs_s.at[d, k - 1, i], recv_sem=rs_r.at[d, k - 1, i],
                device_id=dev(hop if d == 0 else -hop), device_id_type=MESH,
            )

        def rs_sum(d, k, i, value):
            for c in children(k, reach(d, PIECES[i][0])):
                rs_copy(d, c, i).wait_recv()
                value = value + piece(recv.at[d, c - 1], i)[...].astype(F32)
            return value

        def rs_step(d, k, i):
            e, h = PIECES[i]
            piece(send.at[d, k - 1], i)[...] = rs_sum(d, k, i, part_of(block(d, k), e, h)).astype(BF)
            copy = rs_copy(d, k, i)
            copy.start()
            started.append(copy)

        def rs_round(level, expert):
            for k in (4, 3, 2, 1):
                for i, (e, h) in enumerate(PIECES):
                    for d in range(2):
                        n = reach(d, e)
                        if e == expert and k <= n and height(k, n) == level:
                            rs_step(d, k, i)

        def l_copy(d, r):
            return pltpu.make_async_remote_copy(
                src_ref=logit if r == 0 else lrecv.at[d, r - 1], dst_ref=lrecv.at[d, r],
                send_sem=l_s.at[d, r], recv_sem=l_r.at[d, r],
                device_id=dev(1 if d == 0 else -1), device_id_type=MESH,
            )

        def logit_round(r):
            for d in range(2 if r < 3 else 1):
                if r > 0:
                    l_copy(d, r - 1).wait_recv()
                copy = l_copy(d, r)
                copy.start()
                started.append(copy)

        product(0, 0)
        product(1, 0)
        pl.semaphore_wait(barrier, 3)
        rs_round(0, 0)
        product(0, 1)
        product(1, 1)
        product(2, 0)
        product(2, 1)
        product(3, 0)
        product(3, 1)
        g_copy.wait()
        logit[...] = lax.dot_general(
            gate[...], x[...], (((1,), (1,)), ((), ())), preferred_element_type=F32
        )
        logit_round(0)

        rs_round(0, 1)
        for level in range(1, 4):
            rs_round(level, 0)
            rs_round(level, 1)
            logit_round(level)

        def y_copy(i):
            return pltpu.make_async_remote_copy(
                src_ref=piece(ysend, i), dst_ref=piece(yrecv, i), send_sem=y_s.at[i], recv_sem=y_r.at[i],
                device_id=mate, device_id_type=MESH,
            )

        for i, (e, h) in enumerate(PIECES):
            total = part_of(7, e, h)
            for d in (1, 0) if e == 0 else (0, 1):
                total = rs_sum(d, 0, i, total)
            part[3, rows_of(e, h), 128:256] = total
            piece(ysend, i)[...] = total.astype(BF)
            copy = y_copy(i)
            copy.start()
            started.append(copy)

        total = logit[...]
        l_copy(0, 3).wait_recv()
        l_copy(1, 2).wait_recv()
        for d in range(2):
            for r in range(4 - d):
                total = total + lrecv[d, r]
        lsum[...] = total
        l_last = pltpu.make_async_remote_copy(
            src_ref=lsum, dst_ref=lsum_r, send_sem=l_s.at[1, 3], recv_sem=l_r.at[1, 3],
            device_id=mate, device_id_type=MESH,
        )
        l_last.start()
        b_copy.wait()
        for e in range(2):
            acc[e] = jnp.broadcast_to(bias[e : e + 1, :], (256, 512))
        u_copy.wait()

        def ag_copy(d, k, i):
            hop = k - tree[k]
            return pltpu.make_async_remote_copy(
                src_ref=piece(hid if tree[k] == 0 else got.at[d, tree[k] - 1], i),
                dst_ref=piece(got.at[d, k - 1], i),
                send_sem=ag_s.at[d, k - 1, i], recv_sem=ag_r.at[d, k - 1, i],
                device_id=dev(hop if d == 0 else -hop), device_id_type=MESH,
            )

        def forward(d, k, i):
            for c in sorted(children(k, reach(d, PIECES[i][0])), reverse=True):
                copy = ag_copy(d, c, i)
                copy.start()
                started.append(copy)

        def expand(values, e, source):
            wide = jnp.dot(values, pick[e], preferred_element_type=F32).astype(BF)
            rows = pl.ds(pl.multiple_of(source * 256, 256), 256)
            acc[e] += jnp.dot(wide, u[rows, :], preferred_element_type=F32)

        early = list(started)
        for i, (e, h) in enumerate(PIECES):
            y_copy(i).wait_recv()
            piece(hid, i)[...] = jnp.tanh(
                part[3, rows_of(e, h), 128:256] + piece(yrecv, i)[...].astype(F32)
            ).astype(BF)
            for d in range(2):
                forward(d, 0, i)
            if h == CUTS - 1:
                expand(hid[e], e, at(0))

        l_last.wait_recv()
        gating = 1.0 / (1.0 + jnp.exp(-(lsum[...] + lsum_r[...])))
        eye = lax.broadcasted_iota(jnp.int32, (128, 128), 0) == lax.broadcasted_iota(
            jnp.int32, (128, 128), 1
        )

        def sources(level, e):
            for k in (1, 2, 3, 4):
                for d in (0, 1) if e == 0 else (1, 0):
                    if reach(d, e) >= k and depth(k) == level:
                        yield d, k

        def arrive(level, e):
            for d, k in sources(level, e):
                for h in range(CUTS):
                    ag_copy(d, k, CUTS * e + h).wait_recv()
                    forward(d, k, CUTS * e + h)

        def absorb(level, e):
            for d, k in sources(level, e):
                expand(got[d, k - 1, e], e, at(-k if d == 0 else k))

        for level in range(1, 5):
            for e in range(2):
                arrive(level, e)
                absorb(level, e)
                if level == 2:
                    for h in range(2):
                        line = jnp.broadcast_to(gating[e : e + 1, h * 128 : h * 128 + 128], (128, 128))
                        column = jnp.sum(jnp.where(eye, line, 0.0), axis=1, keepdims=True)
                        weight[e, h * 128 : h * 128 + 128, :] = jnp.broadcast_to(column, (128, 128))
            if level == 3:
                for copy in early:
                    copy.wait_send()


        for c in range(4):
            lanes = slice(c * 128, c * 128 + 128)
            blended = weight[0] * acc[0, :, lanes] + weight[1] * acc[1, :, lanes]
            inputs = x[:, lanes].astype(F32)
            out_ref[:, lanes] = (inputs * blended + inputs).astype(BF)

        for copy in started[len(early) :]:
            copy.wait_send()
        l_last.wait_send()

    if TREES[0] == TREES[1]:
        exchange(TREES[0])
    else:
        for c in range(2):
            pl.when(core == c)(functools.partial(exchange, TREES[c]))


def shards(samples, rank_down, rank_up, gate_proj, expert_bias):
    dma = pltpu.SemaphoreType.DMA
    return pl.pallas_call(
        kernel,
        out_shape=pltpu.VMEM(samples.shape, samples.dtype),
        in_specs=[pl.BlockSpec(memory_space=pl.ANY)] * 5,
        out_specs=pl.BlockSpec(memory_space=pltpu.VMEM),
        scratch_shapes=[
            pltpu.VMEM((256, 512), BF),
            pltpu.VMEM((1024, 1024), BF),
            pltpu.VMEM((2048, 512), BF),
            pltpu.VMEM((2, 512), BF),
            pltpu.VMEM((2, 512), F32),
            pltpu.VMEM((512, 1024), BF),
            pltpu.VMEM((4, 512, 256), F32),
            pltpu.VMEM((2, 4, 2, 256, 128), BF),
            pltpu.VMEM((2, 4, 2, 256, 128), BF),
            pltpu.VMEM((2, 256, 128), BF),
            pltpu.VMEM((2, 256, 128), BF),
            pltpu.VMEM((2, 256, 128), BF),
            pltpu.VMEM((2, 4, 2, 256, 128), BF),
            pltpu.VMEM((2, 256), F32),
            pltpu.VMEM((2, 4, 2, 256), F32),
            pltpu.VMEM((2, 256), F32),
            pltpu.VMEM((2, 256), F32),
            pltpu.VMEM((2, 256, 512), F32),
            pltpu.VMEM((2, 256, 128), F32),
            dma(()),
            dma((8,)),
            dma(()),
            dma(()),
            dma(()),
            dma((2, 4, 2 * CUTS)),
            dma((2, 4, 2 * CUTS)),
            dma((2 * CUTS,)),
            dma((2 * CUTS,)),
            dma((2, 4, 2 * CUTS)),
            dma((2, 4, 2 * CUTS)),
            dma((2, 4)),
            dma((2, 4)),
        ],
        compiler_params=pltpu.CompilerParams(collective_id=0, has_side_effects=True),
        name="cross_experts",
    )(samples, rank_down, rank_up, gate_proj.T, expert_bias)


def solution(mesh):
    placed = (
        P("batch", "width"),
        P("width", None, None),
        P(None, None, "width"),
        P("width", None),
        P(None, "width"),
    )
    return jax.shard_map(
        shards, mesh=mesh, in_specs=placed, out_specs=P("batch", "width"), check_vma=False
    )
```

```python
import functools

import jax
import jax.numpy as jnp
from jax import lax
from jax.experimental import pallas as pl
from jax.experimental.pallas import tpu as pltpu
from jax.sharding import PartitionSpec as P

MESH = pl.DeviceIdType.MESH
BF = jnp.bfloat16
F32 = jnp.float32
RING = 8
CUTS = 2
TALL = 256 // CUTS
PIECES = tuple((e, h) for e in range(2) for h in range(CUTS))
ORDER = (4, 3, -3, 2, -2, 1, -1, 0)
TREES = ((0, 0, 1, 2, 3), (0, 0, 1, 2, 3))


def reach(direction, expert):
    return 4 if (direction == 0) == (expert == 0) else 3


def block(d, distance):
    return ORDER.index(distance if d == 0 or distance in (0, 4) else -distance)


def rows_of(e, h):
    return slice(e * 256 + h * TALL, e * 256 + h * TALL + TALL)


def piece(ref, i):
    e, h = PIECES[i]
    return ref.at[e, pl.ds(h * TALL, TALL)]


def kernel(
    x_hbm, w_hbm, u_hbm, gate_hbm, bias_hbm, out_ref,
    x, w, u, gate, bias, xe, part, send, recv, ysend, yrecv, hid, got, logit, lrecv, lsum, lsum_r, acc, weight,
    x_sem, w_sem, u_sem, g_sem, b_sem,
    rs_s, rs_r, y_s, y_r, ag_s, ag_r, l_s, l_r,
):
    me = lax.axis_index("width")
    z = me // 2
    y = lax.rem(me, 2)
    core = lax.rem(lax.axis_index("batch"), 2)

    def at(offset):
        return lax.rem(z + offset + RING, RING)

    def dev(offset):
        return {"width": at(offset) * 2 + y}

    mate = {"width": z * 2 + (1 - y)}

    barrier = pltpu.get_barrier_semaphore()
    x_copy = pltpu.make_async_copy(x_hbm, x, x_sem)
    x_copy.start()
    w_rows = w_hbm.reshape(1024, 1024)
    w_copies = []
    for t, offset in enumerate(ORDER):
        lanes = pl.ds(pl.multiple_of(at(offset) * 128, 128), 128)
        w_copies.append(
            pltpu.make_async_copy(w_rows.at[:, lanes], w.at[:, pl.ds(t * 128, 128)], w_sem.at[t])
        )
        w_copies[-1].start()
    pl.semaphore_signal(barrier, inc=1, device_id=mate, device_id_type=MESH)
    for offset in (1, -1):
        pl.semaphore_signal(barrier, inc=1, device_id=dev(offset), device_id_type=MESH)
    g_copy = pltpu.make_async_copy(gate_hbm, gate, g_sem)
    g_copy.start()
    b_copy = pltpu.make_async_copy(bias_hbm, bias, b_sem)
    b_copy.start()
    u_copy = pltpu.make_async_copy(u_hbm.reshape(2048, 512), u, u_sem)
    u_copy.start()

    row = lax.broadcasted_iota(jnp.int32, (128, 256), 0)
    lane = lax.broadcasted_iota(jnp.int32, (128, 256), 1)
    pick = [jnp.where(lane == 2 * row + e, 1.0, 0.0).astype(BF) for e in range(2)]

    x_copy.wait()
    for e in range(2):
        for c in range(4):
            xe[e * 256 : (e + 1) * 256, c * 256 : (c + 1) * 256] = jnp.dot(
                x[:, c * 128 : (c + 1) * 128], pick[e], preferred_element_type=F32
            ).astype(BF)

    def product(p, e):
        if e == 0:
            w_copies[2 * p].wait()
            w_copies[2 * p + 1].wait()
        rows = slice(e * 256, e * 256 + 256)
        part[p, rows, :] = jnp.dot(
            xe[rows, :], w[:, p * 256 : (p + 1) * 256], preferred_element_type=F32
        )

    def part_of(t, e, h):
        return part[t // 2, rows_of(e, h), (t % 2) * 128 : (t % 2) * 128 + 128]

    def exchange(tree):
        started = []

        def height(k, n):
            below = [height(c, n) + 1 for c in range(1, n + 1) if tree[c] == k]
            return max(below, default=0)

        def depth(k):
            return 0 if k == 0 else depth(tree[k]) + 1

        def children(k, n):
            return [c for c in range(1, n + 1) if tree[c] == k]

        def rs_copy(d, k, i):
            hop = k - tree[k]
            return pltpu.make_async_remote_copy(
                src_ref=piece(send.at[d, k - 1], i), dst_ref=piece(recv.at[d, k - 1], i),
                send_sem=rs_s.at[d, k - 1, i], recv_sem=rs_r.at[d, k - 1, i],
                device_id=dev(hop if d == 0 else -hop), device_id_type=MESH,
            )

        def rs_sum(d, k, i, value):
            for c in children(k, reach(d, PIECES[i][0])):
                rs_copy(d, c, i).wait_recv()
                value = value + piece(recv.at[d, c - 1], i)[...].astype(F32)
            return value

        def rs_step(d, k, i):
            e, h = PIECES[i]
            piece(send.at[d, k - 1], i)[...] = rs_sum(d, k, i, part_of(block(d, k), e, h)).astype(BF)
            copy = rs_copy(d, k, i)
            copy.start()
            started.append(copy)

        def rs_round(level, expert):
            for k in (4, 3, 2, 1):
                for i, (e, h) in enumerate(PIECES):
                    for d in range(2):
                        n = reach(d, e)
                        if e == expert and k <= n and height(k, n) == level:
                            rs_step(d, k, i)

        def l_copy(d, r):
            return pltpu.make_async_remote_copy(
                src_ref=logit if r == 0 else lrecv.at[d, r - 1], dst_ref=lrecv.at[d, r],
                send_sem=l_s.at[d, r], recv_sem=l_r.at[d, r],
                device_id=dev(1 if d == 0 else -1), device_id_type=MESH,
            )

        def logit_round(r):
            for d in range(2 if r < 3 else 1):
                if r > 0:
                    l_copy(d, r - 1).wait_recv()
                copy = l_copy(d, r)
                copy.start()
                started.append(copy)

        product(0, 0)
        product(1, 0)
        pl.semaphore_wait(barrier, 3)
        rs_round(0, 0)
        product(0, 1)
        product(1, 1)
        product(2, 0)
        product(2, 1)
        product(3, 0)
        product(3, 1)
        g_copy.wait()
        logit[...] = lax.dot_general(
            gate[...], x[...], (((1,), (1,)), ((), ())), preferred_element_type=F32
        )
        logit_round(0)

        rs_round(0, 1)
        for level in range(1, 4):
            rs_round(level, 0)
            rs_round(level, 1)
            logit_round(level)

        def y_copy(i):
            return pltpu.make_async_remote_copy(
                src_ref=piece(ysend, i), dst_ref=piece(yrecv, i), send_sem=y_s.at[i], recv_sem=y_r.at[i],
                device_id=mate, device_id_type=MESH,
            )

        for i, (e, h) in enumerate(PIECES):
            total = part_of(7, e, h)
            for d in (1, 0) if e == 0 else (0, 1):
                total = rs_sum(d, 0, i, total)
            part[3, rows_of(e, h), 128:256] = total
            piece(ysend, i)[...] = total.astype(BF)
            copy = y_copy(i)
            copy.start()
            started.append(copy)

        total = logit[...]
        l_copy(0, 3).wait_recv()
        l_copy(1, 2).wait_recv()
        for d in range(2):
            for r in range(4 - d):
                total = total + lrecv[d, r]
        lsum[...] = total
        l_last = pltpu.make_async_remote_copy(
            src_ref=lsum, dst_ref=lsum_r, send_sem=l_s.at[1, 3], recv_sem=l_r.at[1, 3],
            device_id=mate, device_id_type=MESH,
        )
        l_last.start()
        b_copy.wait()
        for e in range(2):
            acc[e] = jnp.broadcast_to(bias[e : e + 1, :], (256, 512))
        u_copy.wait()

        def ag_copy(d, k, i):
            hop = k - tree[k]
            return pltpu.make_async_remote_copy(
                src_ref=piece(hid if tree[k] == 0 else got.at[d, tree[k] - 1], i),
                dst_ref=piece(got.at[d, k - 1], i),
                send_sem=ag_s.at[d, k - 1, i], recv_sem=ag_r.at[d, k - 1, i],
                device_id=dev(hop if d == 0 else -hop), device_id_type=MESH,
            )

        def forward(d, k, i):
            for c in sorted(children(k, reach(d, PIECES[i][0])), reverse=True):
                copy = ag_copy(d, c, i)
                copy.start()
                started.append(copy)

        def expand(values, e, source):
            wide = jnp.dot(values, pick[e], preferred_element_type=F32).astype(BF)
            rows = pl.ds(pl.multiple_of(source * 256, 256), 256)
            acc[e] += jnp.dot(wide, u[rows, :], preferred_element_type=F32)

        early = list(started)
        for i, (e, h) in enumerate(PIECES):
            y_copy(i).wait_recv()
            piece(hid, i)[...] = jnp.tanh(
                part[3, rows_of(e, h), 128:256] + piece(yrecv, i)[...].astype(F32)
            ).astype(BF)
            for d in range(2):
                forward(d, 0, i)
            if h == CUTS - 1:
                expand(hid[e], e, at(0))

        l_last.wait_recv()
        gating = 1.0 / (1.0 + jnp.exp(-(lsum[...] + lsum_r[...])))
        eye = lax.broadcasted_iota(jnp.int32, (128, 128), 0) == lax.broadcasted_iota(
            jnp.int32, (128, 128), 1
        )

        def sources(level, e):
            for k in (1, 2, 3, 4):
                for d in (0, 1) if e == 0 else (1, 0):
                    if reach(d, e) >= k and depth(k) == level:
                        yield d, k

        def arrive(level, e):
            for h in range(CUTS):
                for d, k in sources(level, e):
                    ag_copy(d, k, CUTS * e + h).wait_recv()
                    forward(d, k, CUTS * e + h)

        def absorb(level, e):
            for d, k in sources(level, e):
                expand(got[d, k - 1, e], e, at(-k if d == 0 else k))

        for level in range(1, 5):
            for e in range(2):
                arrive(level, e)
                absorb(level, e)
                if level == 2:
                    for h in range(2):
                        line = jnp.broadcast_to(gating[e : e + 1, h * 128 : h * 128 + 128], (128, 128))
                        column = jnp.sum(jnp.where(eye, line, 0.0), axis=1, keepdims=True)
                        weight[e, h * 128 : h * 128 + 128, :] = jnp.broadcast_to(column, (128, 128))
            if level == 3:
                for copy in early:
                    copy.wait_send()


        for c in range(4):
            lanes = slice(c * 128, c * 128 + 128)
            blended = weight[0] * acc[0, :, lanes] + weight[1] * acc[1, :, lanes]
            inputs = x[:, lanes].astype(F32)
            out_ref[:, lanes] = (inputs * blended + inputs).astype(BF)

        for copy in started[len(early) :]:
            copy.wait_send()
        l_last.wait_send()

    if TREES[0] == TREES[1]:
        exchange(TREES[0])
    else:
        for c in range(2):
            pl.when(core == c)(functools.partial(exchange, TREES[c]))


def shards(samples, rank_down, rank_up, gate_proj, expert_bias):
    dma = pltpu.SemaphoreType.DMA
    return pl.pallas_call(
        kernel,
        out_shape=pltpu.VMEM(samples.shape, samples.dtype),
        in_specs=[pl.BlockSpec(memory_space=pl.ANY)] * 5,
        out_specs=pl.BlockSpec(memory_space=pltpu.VMEM),
        scratch_shapes=[
            pltpu.VMEM((256, 512), BF),
            pltpu.VMEM((1024, 1024), BF),
            pltpu.VMEM((2048, 512), BF),
            pltpu.VMEM((2, 512), BF),
            pltpu.VMEM((2, 512), F32),
            pltpu.VMEM((512, 1024), BF),
            pltpu.VMEM((4, 512, 256), F32),
            pltpu.VMEM((2, 4, 2, 256, 128), BF),
            pltpu.VMEM((2, 4, 2, 256, 128), BF),
            pltpu.VMEM((2, 256, 128), BF),
            pltpu.VMEM((2, 256, 128), BF),
            pltpu.VMEM((2, 256, 128), BF),
            pltpu.VMEM((2, 4, 2, 256, 128), BF),
            pltpu.VMEM((2, 256), F32),
            pltpu.VMEM((2, 4, 2, 256), F32),
            pltpu.VMEM((2, 256), F32),
            pltpu.VMEM((2, 256), F32),
            pltpu.VMEM((2, 256, 512), F32),
            pltpu.VMEM((2, 256, 128), F32),
            dma(()),
            dma((8,)),
            dma(()),
            dma(()),
            dma(()),
            dma((2, 4, 2 * CUTS)),
            dma((2, 4, 2 * CUTS)),
            dma((2 * CUTS,)),
            dma((2 * CUTS,)),
            dma((2, 4, 2 * CUTS)),
            dma((2, 4, 2 * CUTS)),
            dma((2, 4)),
            dma((2, 4)),
        ],
        compiler_params=pltpu.CompilerParams(collective_id=0, has_side_effects=True),
        name="cross_experts",
    )(samples, rank_down, rank_up, gate_proj.T, expert_bias)


def solution(mesh):
    placed = (
        P("batch", "width"),
        P("width", None, None),
        P(None, None, "width"),
        P("width", None),
        P(None, "width"),
    )
    return jax.shard_map(
        shards, mesh=mesh, in_specs=placed, out_specs=P("batch", "width"), check_vma=False
    )
```
